32 devices in a mesh: pipe: 2 (over x), fsdp: 16 (over z, y, core).
Axes of the slice: x: 2, y: 2, z: 4, core: 2. Of those that a mesh axis runs over, the one named last changes fastest.
Arguments:
- x_in: bfloat16 [2, 4096, 1024], P(None, 'fsdp'), may hold values from -6 to 6
- cotangent: bfloat16 [2, 4096, 1024], P(None, 'fsdp'), may hold values from -6 to 6
- segment: int32 [2, 4096], P(None, 'fsdp'), may hold values from 0 to 3, never falling along the last dimension, each value on 1 to 2000 neighbouring positions
- w_qkv: bfloat16 [2, 1024, 3072], P('pipe', 'fsdp'), may hold values from -0.1875 to 0.1875
- w_out: bfloat16 [2, 1024, 1024], P('pipe', 'fsdp'), may hold values from -1 to 1
- w_up: bfloat16 [2, 1024, 4096], P('pipe', 'fsdp'), may hold values from -0.1875 to 0.1875
- w_down: bfloat16 [2, 4096, 1024], P('pipe', 'fsdp'), may hold values from -0.09375 to 0.09375
- vectors: bfloat16 [2, 10240], P('pipe', 'fsdp'), may hold values from -3 to 3
- gains: bfloat16 [2, 2048], P('pipe', 'fsdp'), may hold values from 0.5 to 1.5
Outputs:
- section_out: bfloat16 [2, 2, 4096, 1024], P('pipe', None, 'fsdp')
- section_in_grad: bfloat16 [2, 2, 4096, 1024], P('pipe', None, 'fsdp')
- grad_w_qkv: float32 [2, 1024, 3072], P('pipe', 'fsdp')
- grad_w_out: float32 [2, 1024, 1024], P('pipe', 'fsdp')
- grad_w_up: float32 [2, 1024, 4096], P('pipe', 'fsdp')
- grad_w_down: float32 [2, 4096, 1024], P('pipe', 'fsdp')
- grad_vectors: float32 [2, 10240], P('pipe', 'fsdp')
- grad_gains: float32 [2, 2048], P('pipe', 'fsdp')
The draws below stay inside these ranges and needn't reach their ends.
Inputs may be any that keep to these rules, and one draw needn't show every extreme that they name: `segment`: in each micro-batch the ids never fall; every document has 1 to 2000 tokens and one has exactly 2000.
All inputs are finite; a program needn't handle non-finite values.
Results may differ from the reference program's by a relative error of at most 0.015.
Values may be sent and summed in bfloat16 or wider, within the bound.
No kernel may reach another device: no remote copies, remote signals or barrier semaphores. Data moves between devices by JAX's collectives and lax.ppermute only.
A program may use at most 256 MiB of HBM per device.

```python
import math
import jax
import jax.numpy as jnp
import numpy as np
from jax import lax

D = 1024
H = 16
HD = 64
FF = 4096
MB = 2
DOC_MAX = 2000
SECTIONS = 2
TOKENS = 4096
DOCS = 4
VEC = 10240


def with_spikes(drawn, stream_key, source, target, parts, factor):
    owner, partner = [(jnp.arange(drawn.shape[position]) // (drawn.shape[position] // parts)).reshape([-1 if axis == position else 1 for axis in range(drawn.ndim)]) for position in (source, target)]
    chosen = jax.random.permutation(stream_key, parts)[partner]
    strong = (owner == chosen) | (owner == (partner + parts // 2) % parts)
    return jnp.where(strong, factor * drawn, drawn)


def block_scale(own_key, dims, cuts, smallest, high):
    level, own = 1.0, jax.random.fold_in(own_key, 6)
    for axis_at, blocks in cuts:
        draws = jnp.exp(jax.random.uniform(jax.random.fold_in(own, axis_at), (blocks,), jnp.float32, smallest / len(cuts), high / len(cuts)))
        level = level * jnp.repeat(draws, dims[axis_at] // blocks).reshape([-1 if axis == axis_at else 1 for axis in range(len(dims))])
    return level


def split_up(number_of, total, most, slope):
    portions = [(1 << 20) // math.isqrt(grade ** slope) + 1 for grade in range(2, number_of + 1)]
    surplus, holding = total - most - (number_of - 1), [1] * (number_of - 1)
    while surplus > 0:
        candidates = [i for i in range(number_of - 1) if holding[i] < most]
        mass, left = sum([portions[i] for i in candidates]), surplus
        for i in candidates:
            more = min(most - holding[i], max(1, left * portions[i] // mass), surplus)
            holding[i] = holding[i] + more
            surplus = surplus - more
    return np.array([most] + holding)


def ragged(rng, amount, total, reach, lean):
    if amount == 2:
        one = jax.random.randint(rng, (), max(1, total - reach), min(reach, total - 1) + 1)
        return jnp.stack([one, total - one])
    sizes = jnp.asarray(split_up(amount, total, reach, lean), jnp.int32)
    pairs = (amount - 1) // 2
    giver, sink = sizes[1:1 + 2 * pairs:2], sizes[2:2 + 2 * pairs:2]
    slack = jnp.minimum(giver - 1, reach - sink)
    shifted = jax.random.randint(jax.random.fold_in(rng, 1), (pairs,), 0, 1 << 20) % (slack + 1)
    sizes = sizes.at[1:1 + 2 * pairs:2].set(giver - shifted).at[2:2 + 2 * pairs:2].set(sink + shifted)
    return sizes[jax.random.permutation(jax.random.fold_in(rng, 2), amount)]


def gaussian(key, extent, width, limit, cuts=(), kind=jnp.bfloat16):
    gain = block_scale(key, extent, cuts, -0.22, 0.18) if cuts else 1.0
    result = jax.random.normal(key, extent, jnp.float32) * width * gain
    return jnp.minimum(jnp.maximum(result, -limit), limit).astype(kind)


def heavy_noise(stream_key, shape, spread, reach, cuts, heavy, kind=jnp.bfloat16):
    values = spread * jax.random.normal(stream_key, shape, jnp.float32)
    if cuts:
        values = values * block_scale(stream_key, shape, cuts, -0.22, 0.18)
    return jnp.clip(with_spikes(values, jax.random.fold_in(stream_key, 3), *heavy), -reach, reach).astype(kind)


def setup_inputs(seed: int = 0) -> dict:
    streams_of = jax.random.split(jax.random.key(seed), 10)
    return {
        "x_in": heavy_noise(streams_of[0], (MB, TOKENS, D), 1.0, 6.0, ((1, 16),), (1, 2, 16, 2.0)),
        "cotangent": gaussian(streams_of[1], (MB, TOKENS, D), 1.0, 6.0, ((1, 16),)),
        "segment": jax.vmap(lambda own: jnp.searchsorted(jnp.cumsum(ragged(own, DOCS, TOKENS, DOC_MAX, 1)), jnp.arange(TOKENS), side="right"))(jax.random.split(streams_of[2], MB)).reshape((MB, TOKENS)).astype(jnp.int32),
        "w_qkv": gaussian(streams_of[3], (SECTIONS, D, 3 * D), D ** -0.5, 0.1875, ((0, 2), (1, 16))),
        "w_out": gaussian(streams_of[4], (SECTIONS, D, D), (D // 32) ** -0.5, 1.0, ((0, 2), (1, 16))),
        "w_up": gaussian(streams_of[5], (SECTIONS, D, FF), D ** -0.5, 0.1875, ((0, 2), (1, 16))),
        "w_down": gaussian(streams_of[6], (SECTIONS, FF, D), FF ** -0.5, 0.09375, ((0, 2), (1, 16))),
        "vectors": gaussian(streams_of[7], (SECTIONS, VEC), 0.5, 3.0, ((0, 2), (1, 16))),
        "gains": jnp.clip(1.0 + 0.1 * jax.random.normal(streams_of[8], (SECTIONS, 2 * D), jnp.float32), 0.5, 1.5).astype(jnp.bfloat16),
    }


EPSILON = 1e-05
MASKED_SCORE = -1e+30
HIGHEST = lax.Precision.HIGHEST

@jax.custom_vjp
def low(v):
    return lax.optimization_barrier(v.astype(jnp.bfloat16)).astype(jnp.float32)

@jax.custom_vjp
def low_back(v):
    return v

def low_keep(v):
    return (low(v), None)

def low_pass(kept, grad):
    return (grad,)

def back_keep(v):
    return (v, None)

def back_low(kept, grad):
    return (low(grad),)
low.defvjp(low_keep, low_pass)
low_back.defvjp(back_keep, back_low)

def product(left, right):
    return jnp.dot(left, right, precision=HIGHEST, preferred_element_type=jnp.float32)

def layer_norm(features, scale_vec, shift_vec):
    row_mean = lax.optimization_barrier(jnp.mean(features, axis=-1, keepdims=True))
    centred = features - row_mean
    return centred * lax.rsqrt(lax.optimization_barrier(jnp.mean(centred * centred, axis=-1, keepdims=True)) + EPSILON) * scale_vec + shift_vec

def gelu_tanh(values):
    return jax.nn.gelu(values, approximate=True)

def attention(query, key_rows, value_rows, seg_ids):
    length = query.shape[0]
    block_rows = min(512, length)
    query_heads = query.reshape(length, H, HD)
    key_heads = key_rows.reshape(length, H, HD)
    value_heads = value_rows.reshape(length, H, HD)
    key_place = jnp.arange(length, dtype=jnp.int32)

    def one_block(block_index):
        row_start = block_index * block_rows
        query_rows = lax.dynamic_slice_in_dim(query_heads, row_start, block_rows, 0)
        seg_rows = lax.dynamic_slice_in_dim(seg_ids, row_start, block_rows, 0)
        query_place = row_start + jnp.arange(block_rows, dtype=jnp.int32)
        allowed = (seg_rows[:, None] == seg_ids[None, :]) & (key_place[None, :] <= query_place[:, None])
        scores = low_back(jnp.einsum('thd,uhd->htu', query_rows, key_heads, precision=HIGHEST) * HD ** (-0.5))
        masked = jnp.where(allowed[None], scores, MASKED_SCORE)
        log_total = jax.nn.logsumexp(masked, axis=2, keepdims=True)
        probabilities = low(jnp.where(allowed[None], jnp.exp(masked - log_total), 0.0))
        return jnp.einsum('htu,uhd->thd', probabilities, value_heads, precision=HIGHEST)
    mixed_out = lax.map(jax.checkpoint(one_block), jnp.arange(length // block_rows, dtype=jnp.int32))
    return mixed_out.reshape(length, H * HD)

def section_layer(section_rows, seg_ids, section_params):
    w_qkv, w_out, w_up, w_down, vectors, gains = section_params
    width_all = section_rows.shape[1]
    hidden = w_up.shape[1]
    ln1_shift = vectors[0:width_all]
    ln2_shift = vectors[width_all:2 * width_all]
    q_bias = vectors[2 * width_all:3 * width_all]
    v_bias = vectors[3 * width_all:4 * width_all]
    out_bias = vectors[4 * width_all:5 * width_all]
    up_bias = vectors[5 * width_all:5 * width_all + hidden]
    down_bias = vectors[5 * width_all + hidden:]
    normed_in = low(layer_norm(section_rows, gains[:width_all], ln1_shift))
    qkv_sum = product(normed_in, w_qkv)
    query = low(low_back(qkv_sum[:, :width_all] + q_bias))
    key_rows = low(low_back(qkv_sum[:, width_all:2 * width_all]))
    value_rows = low(low_back(qkv_sum[:, 2 * width_all:] + v_bias))
    mixed_out = low(low_back(attention(query, key_rows, value_rows, seg_ids)))
    residual = section_rows + low_back(product(mixed_out, w_out) + out_bias)
    ffn_in = low(layer_norm(residual, gains[width_all:], ln2_shift))
    up_proj = low_back(product(ffn_in, w_up) + up_bias)
    act_out = low(gelu_tanh(up_proj))
    return residual + low_back(product(act_out, w_down) + down_bias)

def reference(x_in, cotangent, segment, w_qkv, w_out, w_up, w_down, vectors, gains):
    parameters = tuple((param.astype(jnp.float32) for param in (w_qkv, w_out, w_up, w_down, vectors, gains)))
    inputs = x_in.astype(jnp.float32)
    section_probe = jnp.zeros_like(inputs)

    def whole_run(parameters, inputs, section_probe):
        lower_params = tuple((param[0] for param in parameters))
        upper_params = tuple((param[1] for param in parameters))

        def one_batch(batch_items):
            batch_rows, probe_rows, seg_ids = batch_items
            first_out = section_layer(batch_rows, seg_ids, lower_params)
            handed = low(first_out)
            second = section_layer(low_back(handed + probe_rows), seg_ids, upper_params)
            return (handed, second)
        return lax.map(jax.checkpoint(one_batch), (inputs, section_probe, segment))
    (handed, second), pullback = jax.vjp(whole_run, parameters, inputs, section_probe)
    gradients, input_grads, probe_grads = pullback((jnp.zeros_like(handed), cotangent.astype(jnp.float32)))
    section_out = jnp.stack([handed, second]).astype(jnp.bfloat16)
    section_in_grad = jnp.stack([input_grads, probe_grads]).astype(jnp.bfloat16)
    return (section_out, section_in_grad, gradients[0], gradients[1], gradients[2], gradients[3], gradients[4], gradients[5])
```

```python
import functools

import jax
import jax.numpy as jnp
from jax import lax
from jax.experimental import pallas as pl
from jax.experimental.pallas import tpu as pltpu
from jax.sharding import PartitionSpec as P

H = 16
HD = 64
DOC_MAX = 2000

EPSILON = 1e-05
MASKED_SCORE = -1e30


def dot_f32(left, right):
    return jnp.dot(left, right, preferred_element_type=jnp.float32)

def forward_kernel(off, low_ref, qkv_ref, start_ref, o_ref, o32_ref, lse_ref, keys_ref):
    count, _, tokens = qkv_ref.shape

    def turn(j, carry):
        keys_ref[j] = qkv_ref[j, HD : 2 * HD, :].T
        return carry

    lax.fori_loop(0, count, turn, 0)
    sub = lax.broadcasted_iota(jnp.int32, (tokens, tokens), 0)
    lane = lax.broadcasted_iota(jnp.int32, (1, tokens), 1)

    def query_block(i, carry):
        own = i + off
        query = qkv_ref[own, 0:HD, :] * jnp.asarray(HD ** (-0.5), jnp.bfloat16)
        first = start_ref[i]
        place = own * tokens + lane

        def key_block(j, state):
            peak, total, mixed = state
            scores = dot_f32(keys_ref[j], query)
            key_place = sub + j * tokens
            allowed = (key_place >= first) & (key_place <= place)
            scores = jnp.where(allowed, scores, MASKED_SCORE)
            raised = jnp.maximum(peak, jnp.max(scores, axis=0, keepdims=True))
            weights = jnp.exp(scores - raised)
            fade = jnp.exp(peak - raised)
            total = total * fade + jnp.sum(weights, axis=0, keepdims=True)
            mixed = mixed * fade + dot_f32(qkv_ref[j, 2 * HD : 3 * HD, :], weights.astype(jnp.bfloat16))
            return raised, total, mixed

        peak, total, mixed = lax.fori_loop(
            low_ref[i],
            own + 1,
            key_block,
            (
                jnp.full((1, tokens), MASKED_SCORE, jnp.float32),
                jnp.zeros((1, tokens), jnp.float32),
                jnp.zeros((HD, tokens), jnp.float32),
            ),
        )
        out = mixed / total
        o32_ref[i] = out
        o_ref[i] = out.astype(jnp.bfloat16)
        lse_ref[i] = peak + jnp.log(total)
        return carry

    lax.fori_loop(0, count - off, query_block, 0)


def attend(qkv, starts, low, off):
    count, _, tokens = qkv.shape
    rows = count - off
    vmem = pl.BlockSpec(memory_space=pltpu.VMEM)
    return pl.pallas_call(
        functools.partial(forward_kernel, off),
        out_shape=(
            jax.ShapeDtypeStruct((rows, HD, tokens), jnp.bfloat16),
            jax.ShapeDtypeStruct((rows, HD, tokens), jnp.float32),
            jax.ShapeDtypeStruct((rows, 1, tokens), jnp.float32),
        ),
        in_specs=[pl.BlockSpec(memory_space=pltpu.SMEM), vmem, vmem],
        out_specs=(vmem, vmem, vmem),
        scratch_shapes=[pltpu.VMEM((count, tokens, HD), jnp.bfloat16)],
        name="attend",
    )(low, qkv, starts)


def backward_kernel(off, low_ref, high_ref, qkv_ref, start_ref, do_ref, o32_ref, lse_ref,
                    out_ref, keys_ref, values_ref, query_ref, grad_ref, delta_ref, dq_ref):
    count, _, tokens = qkv_ref.shape
    scale = jnp.asarray(HD ** (-0.5), jnp.bfloat16)

    def turn(j, carry):
        keys_ref[j] = qkv_ref[j, HD : 2 * HD, :].T
        values_ref[j] = qkv_ref[j, 2 * HD : 3 * HD, :].T
        return carry

    def turn_query(i, carry):
        query_ref[i] = (qkv_ref[i + off, 0:HD, :] * scale).T
        grad = do_ref[i]
        grad_ref[i] = grad.T
        delta_ref[i] = jnp.sum(grad.astype(jnp.float32) * o32_ref[i], axis=0, keepdims=True)
        dq_ref[i] = jnp.zeros((HD, tokens), jnp.float32)
        return carry

    lax.fori_loop(0, count, turn, 0)
    lax.fori_loop(0, count - off, turn_query, 0)
    sub = lax.broadcasted_iota(jnp.int32, (tokens, tokens), 0)
    lane = lax.broadcasted_iota(jnp.int32, (1, tokens), 1)

    def key_block(j, carry):
        key_place = sub + j * tokens

        def query_block(i, state):
            dk, dv = state
            query = qkv_ref[i + off, 0:HD, :] * scale
            scores = dot_f32(keys_ref[j], query)
            place = (i + off) * tokens + lane
            allowed = (key_place >= start_ref[i]) & (key_place <= place)
            probs = jnp.where(allowed, jnp.exp(scores - lse_ref[i]), 0.0)
            dprobs = dot_f32(values_ref[j], do_ref[i])
            dscores = (probs * (dprobs - delta_ref[i])).astype(jnp.bfloat16)
            dv = dv + dot_f32(probs.astype(jnp.bfloat16), grad_ref[i])
            dk = dk + dot_f32(dscores, query_ref[i])
            dq_ref[i] = dq_ref[i] + dot_f32(qkv_ref[j, HD : 2 * HD, :], dscores)
            return dk, dv

        zero = jnp.zeros((tokens, HD), jnp.float32)
        dk, dv = lax.fori_loop(jnp.maximum(j - off, 0), high_ref[j] + 1, query_block, (zero, zero))
        out_ref[j, HD : 2 * HD, :] = dk.T.astype(jnp.bfloat16)
        out_ref[j, 2 * HD : 3 * HD, :] = dv.T.astype(jnp.bfloat16)
        return carry

    lax.fori_loop(0, count, key_block, 0)

    def finish(i, carry):
        out_ref[i + off, 0:HD, :] = (dq_ref[i] * HD ** (-0.5)).astype(jnp.bfloat16)
        return carry

    lax.fori_loop(0, count - off, finish, 0)


def attend_back(qkv, starts, low, high, do, o32, lse, off):
    count, _, tokens = qkv.shape
    rows = count - off
    vmem = pl.BlockSpec(memory_space=pltpu.VMEM)
    smem = pl.BlockSpec(memory_space=pltpu.SMEM)
    return pl.pallas_call(
        functools.partial(backward_kernel, off),
        out_shape=jax.ShapeDtypeStruct((count, 3 * HD, tokens), jnp.bfloat16),
        in_specs=[smem, smem, vmem, vmem, vmem, vmem, vmem],
        out_specs=vmem,
        scratch_shapes=[
            pltpu.VMEM((count, tokens, HD), jnp.bfloat16),
            pltpu.VMEM((count, tokens, HD), jnp.bfloat16),
            pltpu.VMEM((rows, tokens, HD), jnp.bfloat16),
            pltpu.VMEM((rows, tokens, HD), jnp.bfloat16),
            pltpu.VMEM((rows, 1, tokens), jnp.float32),
            pltpu.VMEM((rows, HD, tokens), jnp.float32),
        ],
        name="attend_back",
    )(low, high, qkv, starts, do, o32, lse)


def gelu_tanh(values):
    return jax.nn.gelu(values, approximate=True)


def layer_norm(features, scale_vec, shift_vec):
    row_mean = jnp.mean(features, axis=-1, keepdims=True)
    centred = features - row_mean
    scaled = lax.rsqrt(jnp.mean(centred * centred, axis=-1, keepdims=True) + EPSILON)
    normed = centred * scaled
    return (normed * scale_vec + shift_vec, normed, scaled)


def norm_back(incoming, normed, scaled, scale_vec):
    dnormed = incoming * scale_vec
    inner_term = (
        dnormed
        - jnp.mean(dnormed, axis=-1, keepdims=True)
        - normed * jnp.mean(dnormed * normed, axis=-1, keepdims=True)
    )
    return (scaled * inner_term, jnp.sum(incoming * normed, axis=0), jnp.sum(incoming, axis=0))


def contract(left, right, left_dim, right_dim):
    dims = (((left_dim,), (right_dim,)), ((), ()))
    return lax.dot_general(left, right, dims, preferred_element_type=jnp.float32)


def swap(value):
    return lax.ppermute(value, "pipe", [(0, 1), (1, 0)])


def head_groups():
    count = lax.axis_size("fsdp")
    if count == H:
        return None
    return [list(range(first, first + H)) for first in range(0, count, H)]


def exchange(blocks):
    return lax.all_to_all(blocks, "fsdp", 0, 0, axis_index_groups=head_groups(), tiled=True)


def halo_count():
    return 0 if lax.axis_size("fsdp") == H else H


def from_group(value, distance):
    count = lax.axis_size("fsdp")
    route = [(i, i + distance * H) for i in range(count) if 0 <= i + distance * H < count]
    return lax.ppermute(value, "fsdp", route)


def doc_tables(segments, fsdp_index):
    count, tokens = segments.shape
    halo = halo_count()
    group = fsdp_index // H
    own = lax.dynamic_slice_in_dim(segments, group * H, H, 0)
    held = own
    if halo:
        before = lax.dynamic_slice_in_dim(segments, jnp.maximum(group - 1, 0) * H, H, 0)
        before = jnp.where(group > 0, before, -1)
        held = jnp.concatenate([before, own])
    held = held.reshape(1, -1)
    starts = jnp.sum((held < own.reshape(-1, 1)).astype(jnp.int32), axis=1).reshape(H, 1, tokens)
    low = starts[:, 0, 0] // tokens
    blocks = jnp.arange(halo + H, dtype=jnp.int32)
    high = jnp.sum((low[None, :] <= blocks[:, None]).astype(jnp.int32), axis=1) - 1
    return starts, low, high


def section_forward(features_in, weights, tables):
    w_qkv, w_out, w_up, w_down, vectors, gains = weights
    width = features_in.shape[1]
    tokens = features_in.shape[0]
    starts, low, high = tables
    halo = halo_count()
    attn_in, normed_one, scaled_one = layer_norm(features_in, gains[:width], vectors["ln1"])
    attn_low = attn_in.astype(jnp.bfloat16)
    bias = jnp.concatenate([vectors["q"], jnp.zeros_like(vectors["q"]), vectors["v"]])
    qkv = (contract(w_qkv, attn_low, 0, 1) + bias[:, None]).astype(jnp.bfloat16)
    qkv = qkv.reshape(3, H, HD, tokens).transpose(1, 0, 2, 3).reshape(H, 3 * HD, tokens)
    qkv = exchange(qkv)
    if halo:
        qkv = jnp.concatenate([from_group(qkv, 1), qkv])
    mixed, mixed_f32, lse = attend(qkv, starts, low, halo)
    mixed = exchange(mixed).reshape(H * HD, tokens)
    residual = features_in + (contract(mixed, w_out, 0, 0) + vectors["out"])
    ffn_in, normed_two, scaled_two = layer_norm(residual, gains[width:], vectors["ln2"])
    ffn_low = ffn_in.astype(jnp.bfloat16)
    ffn_other = swap(ffn_low)
    ffn_both = jnp.concatenate([ffn_low, ffn_other])
    up_proj = contract(ffn_both, w_up, 1, 0) + vectors["up"]
    act_low = gelu_tanh(up_proj).astype(jnp.bfloat16)
    down = contract(act_low, w_down, 1, 0)
    arrived = swap(down[tokens:].astype(jnp.bfloat16)).astype(jnp.float32)
    result = residual + (down[:tokens] + arrived + vectors["down"])
    kept = {
        "normed_one": normed_one,
        "scaled_one": scaled_one,
        "attn_low": attn_low,
        "qkv": qkv,
        "mixed": mixed,
        "mixed_f32": mixed_f32,
        "lse": lse,
        "normed_two": normed_two,
        "scaled_two": scaled_two,
        "ffn_both": ffn_both,
        "up_proj": up_proj,
        "act_low": act_low,
    }
    return result, kept


def scatter(grad):
    return lax.psum_scatter(grad.astype(jnp.bfloat16), "fsdp", scatter_dimension=0, tiled=True)


def section_backward(incoming, incoming_other, kept, weights, tables):
    w_qkv, w_out, w_up, w_down, vectors, gains = weights
    tokens, width = incoming.shape
    starts, low, high = tables
    halo = halo_count()
    both = jnp.concatenate([incoming, incoming_other])
    act_grad = contract(both, w_down, 1, 1)
    unused_value, gelu_pull = jax.vjp(gelu_tanh, kept["up_proj"])
    up_low = gelu_pull(act_grad)[0].astype(jnp.bfloat16)
    partial = contract(up_low, w_up, 1, 1)
    arrived = swap(partial[tokens:].astype(jnp.bfloat16)).astype(jnp.float32)
    ffn_grad = partial[:tokens] + arrived
    grad_down = scatter(contract(kept["act_low"], both, 0, 0))
    grad_up = contract(kept["ffn_both"], up_low, 0, 0).astype(jnp.bfloat16)
    resid_norm, gain_two, shift_two = norm_back(
        ffn_grad, kept["normed_two"], kept["scaled_two"], gains[width:]
    )
    resid_grad = incoming.astype(jnp.float32) + resid_norm
    proj_low = resid_grad.astype(jnp.bfloat16)
    mixed_grad = contract(w_out, proj_low, 1, 1).astype(jnp.bfloat16)
    mixed_grad = exchange(mixed_grad.reshape(H, HD, tokens))
    grad_out = contract(kept["mixed"], proj_low, 1, 0).astype(jnp.bfloat16)
    grad_mid = scatter(jnp.concatenate([grad_out, grad_up], axis=1))
    dqkv = attend_back(
        kept["qkv"], starts, low, high, mixed_grad, kept["mixed_f32"], kept["lse"], halo
    )
    if halo:
        behind = from_group(dqkv[:halo], -1).astype(jnp.float32)
        behind = behind.at[:, :HD].set(0.0)
        dqkv = (dqkv[halo:].astype(jnp.float32) + behind).astype(jnp.bfloat16)
    dqkv = exchange(dqkv)
    dqkv = dqkv.reshape(H, 3, HD, tokens).transpose(1, 0, 2, 3).reshape(3 * H * HD, tokens)
    attn_grad = contract(dqkv, w_qkv, 0, 1)
    grad_qkv = scatter(contract(kept["attn_low"], dqkv, 0, 1))
    qkv_bias = jnp.sum(dqkv, axis=1, dtype=jnp.float32)
    input_norm, gain_one, shift_one = norm_back(
        attn_grad, kept["normed_one"], kept["scaled_one"], gains[:width]
    )
    vector_grad = {
        "ln1": shift_one,
        "ln2": shift_two,
        "q": qkv_bias[:width],
        "v": qkv_bias[2 * width :],
        "out": jnp.sum(proj_low, axis=0, dtype=jnp.float32),
        "up": jnp.sum(up_low, axis=0, dtype=jnp.float32),
        "down": jnp.sum(incoming, axis=0, dtype=jnp.float32),
        "gains": jnp.concatenate([gain_one, gain_two]),
    }
    return resid_grad + input_norm, (grad_qkv, grad_mid, grad_down), vector_grad


def body(x_in, cotangent, segment, w_qkv, w_out, w_up, w_down, vectors, gains):
    pipe_index = lax.axis_index("pipe")
    fsdp_index = lax.axis_index("fsdp")
    count = lax.axis_size("fsdp")
    first = pipe_index == 0
    batches, tokens, width = x_in.shape
    hidden = w_up.shape[2]
    half = hidden // count // 2

    def mine(pair):
        return jnp.where(first, pair[0], pair[1])

    def other(pair):
        return jnp.where(first, pair[1], pair[0])

    def by_section(own, received):
        return jnp.where(first, own, received), jnp.where(first, received, own)

    up_halves = w_up[0].reshape(-1, count, 2, half)
    up_halves = [up_halves[:, :, side].reshape(-1, count * half) for side in range(2)]
    down_halves = [w_down[0, :half], w_down[0, half:]]
    small = jnp.concatenate([vectors[0], gains[0]])
    qkv_shards = by_section(w_qkv[0], swap(w_qkv[0]))
    mid_own = jnp.concatenate([w_out[0], mine(up_halves)], axis=1)
    mid_sent = jnp.concatenate([w_out[0], other(up_halves)], axis=1)
    mid_shards = by_section(mid_own, swap(mid_sent))
    down_shards = by_section(mine(down_halves), swap(other(down_halves)))
    small_shards = by_section(small, swap(small))

    seg_own = mine((segment[0], segment[1]))
    packed = jnp.concatenate([small_shards[0], small_shards[1], seg_own.astype(jnp.bfloat16)])
    packed = lax.all_gather(packed, "fsdp")
    lengths = small.shape[0]
    vec_rows = vectors.shape[1]
    segments = packed[:, 2 * lengths :].astype(jnp.int32)
    tables = doc_tables(segments, fsdp_index)

    def section_weights(section):
        piece = packed[:, section * lengths : (section + 1) * lengths].astype(jnp.float32)
        flat = piece[:, :vec_rows].reshape(-1)
        up_bias = flat[5 * width : 5 * width + hidden].reshape(count, 2, half)
        named = {
            "ln1": flat[:width],
            "ln2": flat[width : 2 * width],
            "q": flat[2 * width : 3 * width],
            "v": flat[3 * width : 4 * width],
            "out": flat[4 * width : 5 * width],
            "up": mine((up_bias[:, 0].reshape(-1), up_bias[:, 1].reshape(-1))),
            "down": flat[5 * width + hidden :],
        }
        gain_all = piece[:, vec_rows:].reshape(-1)
        full_qkv = lax.all_gather(qkv_shards[section], "fsdp", axis=0, tiled=True)
        full_mid = lax.all_gather(mid_shards[section], "fsdp", axis=0, tiled=True)
        full_down = lax.all_gather(down_shards[section], "fsdp", axis=0, tiled=True)
        return full_qkv, full_mid[:, :width], full_mid[:, width:], full_down, named, gain_all

    weights = [section_weights(0), section_weights(1)]
    start = mine((x_in[0], x_in[1])).astype(jnp.float32)
    result_zero, kept_zero = section_forward(start, weights[0], tables)
    low_zero = result_zero.astype(jnp.bfloat16)
    result_one, kept_one = section_forward(low_zero.astype(jnp.float32), weights[1], tables)
    low_one = result_one.astype(jnp.bfloat16)

    pair = (cotangent[0], cotangent[1])
    grad_one, params_one, vecs_one = section_backward(
        mine(pair), other(pair), kept_one, weights[1], tables
    )
    grad_one = grad_one.astype(jnp.bfloat16)
    grad_zero, params_zero, vecs_zero = section_backward(
        grad_one, swap(grad_one), kept_zero, weights[0], tables
    )
    grad_zero = grad_zero.astype(jnp.bfloat16)

    def both_batches(zero, one):
        kept_rows = mine((zero, one))
        came = swap(other((zero, one)))
        return jnp.stack([jnp.where(first, kept_rows, came), jnp.where(first, came, kept_rows)])[None]

    section_out = both_batches(low_zero, low_one)
    section_in_grad = both_batches(grad_zero, grad_one)

    def owned(zero, one):
        return mine((zero, one)), swap(other((zero, one)))

    qkv_mine, qkv_came = owned(params_zero[0], params_one[0])
    mid_mine, mid_came = owned(params_zero[1], params_one[1])
    down_mine, down_came = owned(params_zero[2], params_one[2])
    grad_qkv = qkv_mine.astype(jnp.float32) + qkv_came.astype(jnp.float32)
    grad_out = mid_mine[:, :width].astype(jnp.float32) + mid_came[:, :width].astype(jnp.float32)

    def woven(kept_half, came_half):
        return jnp.where(first, kept_half, came_half), jnp.where(first, came_half, kept_half)

    rows = w_up.shape[1]
    up_pair = woven(mid_mine[:, width:], mid_came[:, width:])
    grad_up = jnp.stack([part.reshape(rows, count, half) for part in up_pair], axis=2)
    grad_up = grad_up.reshape(rows, hidden).astype(jnp.float32)
    grad_down = jnp.concatenate(woven(down_mine, down_came)).astype(jnp.float32)

    def flat_vectors(named):
        up_half = named["up"].reshape(count, half)
        blank = jnp.zeros_like(up_half)
        up_all = jnp.stack([jnp.where(first, up_half, blank), jnp.where(first, blank, up_half)], axis=1)
        flat = jnp.concatenate(
            [named[key] for key in ("ln1", "ln2", "q", "v", "out")] + [up_all.reshape(-1), named["down"]]
        )
        return jnp.concatenate([flat.reshape(count, -1), named["gains"].reshape(count, -1)], axis=1)

    small_grads = jnp.concatenate([flat_vectors(vecs_zero), flat_vectors(vecs_one)], axis=1)
    small_grads = jnp.sum(lax.all_to_all(small_grads, "fsdp", 0, 0, tiled=True), axis=0)
    small_mine, small_came = owned(small_grads[:lengths], small_grads[lengths:])
    small_total = small_mine + small_came
    return (
        section_out,
        section_in_grad,
        grad_qkv[None],
        grad_out[None],
        grad_up[None],
        grad_down[None],
        small_total[None, :vec_rows],
        small_total[None, vec_rows:],
    )


def solution(mesh):
    return jax.shard_map(
        body,
        mesh=mesh,
        in_specs=(
            P(None, "fsdp", None),
            P(None, "fsdp", None),
            P(None, "fsdp"),
            P("pipe", "fsdp", None),
            P("pipe", "fsdp", None),
            P("pipe", "fsdp", None),
            P("pipe", "fsdp", None),
            P("pipe", "fsdp"),
            P("pipe", "fsdp"),
        ),
        out_specs=(
            P("pipe", None, "fsdp", None),
            P("pipe", None, "fsdp", None),
            P("pipe", "fsdp", None),
            P("pipe", "fsdp", None),
            P("pipe", "fsdp", None),
            P("pipe", "fsdp", None),
            P("pipe", "fsdp"),
            P("pipe", "fsdp"),
        ),
        check_vma=False,
    )
```

```python
import functools

import jax
import jax.numpy as jnp
from jax import lax
from jax.experimental import pallas as pl
from jax.experimental.pallas import tpu as pltpu
from jax.sharding import PartitionSpec as P


H = 16
HD = 64

EPSILON = 1e-05
MASKED_SCORE = -1e30


def dot_f32(left, right):
    return jnp.dot(left, right, preferred_element_type=jnp.float32)


STRIDE = 4


def forward_kernel(off, low_ref, qkv_ref, start_ref, o_ref, o32_ref, lse_ref, keys_ref):
    count, _, tokens = qkv_ref.shape
    span = STRIDE * tokens

    def turn(j, carry):
        keys_ref[pl.ds(pl.multiple_of(j * tokens, tokens), tokens), :] = qkv_ref[j, HD : 2 * HD, :].T
        return carry

    lax.fori_loop(0, count, turn, 0)
    sub = lax.broadcasted_iota(jnp.int32, (span, tokens), 0)
    lane = lax.broadcasted_iota(jnp.int32, (1, tokens), 1)

    def query_block(i, carry):
        own = i + off
        query = qkv_ref[own, 0:HD, :] * jnp.asarray(HD ** (-0.5), jnp.bfloat16)
        first = start_ref[i]
        place = own * tokens + lane
        trips = (own + STRIDE - low_ref[i]) // STRIDE

        def key_blocks(trip, state):
            peak, total, mixed = state
            block = jnp.minimum(low_ref[i] + trip * STRIDE, count - STRIDE)
            rows = pl.multiple_of(block * tokens, tokens)
            scores = dot_f32(keys_ref[pl.ds(rows, span), :], query)
            key_place = sub + block * tokens
            least = jnp.maximum(first, (low_ref[i] + trip * STRIDE) * tokens)
            allowed = (key_place >= least) & (key_place <= place)
            scores = jnp.where(allowed, scores, MASKED_SCORE)
            raised = jnp.maximum(peak, jnp.max(scores, axis=0, keepdims=True))
            weights = jnp.exp(scores - raised)
            fade = jnp.exp(peak - raised)
            total = total * fade + jnp.sum(weights, axis=0, keepdims=True)
            low = weights.astype(jnp.bfloat16)
            mixed = mixed * fade
            for part in range(STRIDE):
                values = qkv_ref[block + part, 2 * HD : 3 * HD, :]
                mixed = mixed + dot_f32(values, low[part * tokens : (part + 1) * tokens])
            return raised, total, mixed

        peak, total, mixed = lax.fori_loop(
            0,
            trips,
            key_blocks,
            (
                jnp.full((1, tokens), MASKED_SCORE, jnp.float32),
                jnp.zeros((1, tokens), jnp.float32),
                jnp.zeros((HD, tokens), jnp.float32),
            ),
        )
        out = mixed / total
        o32_ref[i] = out
        o_ref[i] = out.astype(jnp.bfloat16)
        lse_ref[i] = peak + jnp.log(total)
        return carry

    lax.fori_loop(0, count - off, query_block, 0)


def attend(qkv, starts, low, off):
    count, _, tokens = qkv.shape
    rows = count - off
    vmem = pl.BlockSpec(memory_space=pltpu.VMEM)
    return pl.pallas_call(
        functools.partial(forward_kernel, off),
        out_shape=(
            jax.ShapeDtypeStruct((rows, HD, tokens), jnp.bfloat16),
            jax.ShapeDtypeStruct((rows, HD, tokens), jnp.float32),
            jax.ShapeDtypeStruct((rows, 1, tokens), jnp.float32),
        ),
        in_specs=[pl.BlockSpec(memory_space=pltpu.SMEM), vmem, vmem],
        out_specs=(vmem, vmem, vmem),
        scratch_shapes=[pltpu.VMEM((count * tokens, HD), jnp.bfloat16)],
        name="attend",
    )(low, qkv, starts)


def backward_kernel(off, low_ref, high_ref, qkv_ref, start_ref, do_ref, o32_ref, lse_ref,
                    out_ref, keys_ref, values_ref, query_ref, grad_ref, delta_ref, dq_ref):
    count, _, tokens = qkv_ref.shape
    scale = jnp.asarray(HD ** (-0.5), jnp.bfloat16)

    def turn(j, carry):
        keys_ref[j] = qkv_ref[j, HD : 2 * HD, :].T
        values_ref[j] = qkv_ref[j, 2 * HD : 3 * HD, :].T
        return carry

    def turn_query(i, carry):
        query_ref[i] = (qkv_ref[i + off, 0:HD, :] * scale).T
        grad = do_ref[i]
        grad_ref[i] = grad.T
        delta_ref[i] = jnp.sum(grad.astype(jnp.float32) * o32_ref[i], axis=0, keepdims=True)
        dq_ref[i] = jnp.zeros((HD, tokens), jnp.float32)
        return carry

    lax.fori_loop(0, count, turn, 0)
    lax.fori_loop(0, count - off, turn_query, 0)
    sub = lax.broadcasted_iota(jnp.int32, (tokens, tokens), 0)
    lane = lax.broadcasted_iota(jnp.int32, (1, tokens), 1)

    def key_block(j, carry):
        key_place = sub + j * tokens

        def query_block(i, state):
            dk, dv = state
            query = qkv_ref[i + off, 0:HD, :] * scale
            scores = dot_f32(keys_ref[j], query)
            place = (i + off) * tokens + lane
            allowed = (key_place >= start_ref[i]) & (key_place <= place)
            probs = jnp.where(allowed, jnp.exp(scores - lse_ref[i]), 0.0)
            dprobs = dot_f32(values_ref[j], do_ref[i])
            dscores = (probs * (dprobs - delta_ref[i])).astype(jnp.bfloat16)
            dv = dv + dot_f32(probs.astype(jnp.bfloat16), grad_ref[i])
            dk = dk + dot_f32(dscores, query_ref[i])
            dq_ref[i] = dq_ref[i] + dot_f32(qkv_ref[j, HD : 2 * HD, :], dscores)
            return dk, dv

        zero = jnp.zeros((tokens, HD), jnp.float32)
        dk, dv = lax.fori_loop(jnp.maximum(j - off, 0), high_ref[j] + 1, query_block, (zero, zero))
        out_ref[j, HD : 2 * HD, :] = dk.T.astype(jnp.bfloat16)
        out_ref[j, 2 * HD : 3 * HD, :] = dv.T.astype(jnp.bfloat16)
        return carry

    lax.fori_loop(0, count, key_block, 0)

    def finish(i, carry):
        out_ref[i + off, 0:HD, :] = (dq_ref[i] * HD ** (-0.5)).astype(jnp.bfloat16)
        return carry

    lax.fori_loop(0, count - off, finish, 0)


def attend_back(qkv, starts, low, high, do, o32, lse, off):
    count, _, tokens = qkv.shape
    rows = count - off
    vmem = pl.BlockSpec(memory_space=pltpu.VMEM)
    smem = pl.BlockSpec(memory_space=pltpu.SMEM)
    return pl.pallas_call(
        functools.partial(backward_kernel, off),
        out_shape=jax.ShapeDtypeStruct((count, 3 * HD, tokens), jnp.bfloat16),
        in_specs=[smem, smem, vmem, vmem, vmem, vmem, vmem],
        out_specs=vmem,
        scratch_shapes=[
            pltpu.VMEM((count, tokens, HD), jnp.bfloat16),
            pltpu.VMEM((count, tokens, HD), jnp.bfloat16),
            pltpu.VMEM((rows, tokens, HD), jnp.bfloat16),
            pltpu.VMEM((rows, tokens, HD), jnp.bfloat16),
            pltpu.VMEM((rows, 1, tokens), jnp.float32),
            pltpu.VMEM((rows, HD, tokens), jnp.float32),
        ],
        name="attend_back",
    )(low, high, qkv, starts, do, o32, lse)


def gelu_tanh(values):
    return jax.nn.gelu(values, approximate=True)


def layer_norm(features, scale_vec, shift_vec):
    row_mean = jnp.mean(features, axis=-1, keepdims=True)
    centred = features - row_mean
    scaled = lax.rsqrt(jnp.mean(centred * centred, axis=-1, keepdims=True) + EPSILON)
    normed = centred * scaled
    return (normed * scale_vec + shift_vec, normed, scaled)


def norm_back(incoming, normed, scaled, scale_vec):
    dnormed = incoming * scale_vec
    inner_term = (
        dnormed
        - jnp.mean(dnormed, axis=-1, keepdims=True)
        - normed * jnp.mean(dnormed * normed, axis=-1, keepdims=True)
    )
    return (scaled * inner_term, jnp.sum(incoming * normed, axis=0), jnp.sum(incoming, axis=0))


def contract(left, right, left_dim, right_dim):
    dims = (((left_dim,), (right_dim,)), ((), ()))
    return lax.dot_general(left, right, dims, preferred_element_type=jnp.float32)


def swap(value):
    return lax.ppermute(value, "pipe", [(0, 1), (1, 0)])


def head_groups():
    count = lax.axis_size("fsdp")
    if count == H:
        return None
    return [list(range(first, first + H)) for first in range(0, count, H)]


def exchange(blocks):
    return lax.all_to_all(blocks, "fsdp", 0, 0, axis_index_groups=head_groups(), tiled=True)


def halo_count():
    return 0 if lax.axis_size("fsdp") == H else H


def from_group(value, distance):
    count = lax.axis_size("fsdp")
    route = [(i, i + distance * H) for i in range(count) if 0 <= i + distance * H < count]
    return lax.ppermute(value, "fsdp", route)


def doc_tables(segments, fsdp_index):
    _, tokens = segments.shape
    halo = halo_count()
    group = fsdp_index // H
    own = lax.dynamic_slice_in_dim(segments, group * H, H, 0)
    held = own
    if halo:
        before = lax.dynamic_slice_in_dim(segments, jnp.maximum(group - 1, 0) * H, H, 0)
        before = jnp.where(group > 0, before, -1)
        held = jnp.concatenate([before, own])
    held = held.reshape(1, -1)
    starts = jnp.sum((held < own.reshape(-1, 1)).astype(jnp.int32), axis=1).reshape(H, 1, tokens)
    low = starts[:, 0, 0] // tokens
    blocks = jnp.arange(halo + H, dtype=jnp.int32)
    high = jnp.sum((low[None, :] <= blocks[:, None]).astype(jnp.int32), axis=1) - 1
    return starts, low, high


def by_head(columns, tokens):
    return columns.reshape(3, H, HD, tokens).transpose(1, 0, 2, 3).reshape(H, 3 * HD, tokens)


def from_heads(blocks, tokens):
    return blocks.reshape(H, 3, HD, tokens).transpose(1, 0, 2, 3).reshape(3 * H * HD, tokens)


def heads_from_tokens(attn_low, w_qkv, vectors):
    bias = jnp.concatenate([vectors["q"], jnp.zeros_like(vectors["q"]), vectors["v"]])
    qkv = (contract(w_qkv, attn_low, 0, 1) + bias[:, None]).astype(jnp.bfloat16)
    return exchange(by_head(qkv, attn_low.shape[0]))


def spread_head_columns(shard):
    rows = shard.shape[0]
    blocks = by_head(shard.T, rows)
    copies = lax.axis_size("fsdp") // H
    blocks = jnp.concatenate([blocks] * copies)
    blocks = lax.all_to_all(blocks, "fsdp", 0, 0, tiled=True)
    return blocks.transpose(1, 0, 2).reshape(3 * HD, -1)


def collect_head_columns(grad, small):
    count = lax.axis_size("fsdp")
    blocks = grad.reshape(3 * HD, count, -1).transpose(1, 0, 2).astype(jnp.bfloat16)
    rows = blocks.shape[2]
    packed = small.astype(jnp.bfloat16).reshape(count, -1, rows)
    blocks = jnp.concatenate([blocks, packed], axis=1)
    blocks = lax.all_to_all(blocks, "fsdp", 0, 0, tiled=True)
    small = jnp.sum(blocks[:, 3 * HD :].astype(jnp.float32), axis=0).reshape(-1)
    blocks = blocks[:, : 3 * HD].reshape(count // H, H, 3 * HD, rows)
    if count > H:
        blocks = jnp.sum(blocks.astype(jnp.float32), axis=0).astype(jnp.bfloat16)
    return from_heads(blocks.reshape(H, 3 * HD, rows), rows).T, small


def heads_of_group(attn_all, w_head, vectors, head):
    bias = jnp.stack([vectors["q"], jnp.zeros_like(vectors["q"]), vectors["v"]])
    bias = lax.dynamic_index_in_dim(bias.reshape(3, H, HD), head, 1, keepdims=False).reshape(-1)
    blocks, tokens, width = attn_all.shape
    qkv = contract(w_head, attn_all.reshape(blocks * tokens, width), 1, 1) + bias[:, None]
    return qkv.astype(jnp.bfloat16).reshape(3 * HD, blocks, tokens).transpose(1, 0, 2)


def section_forward(features_in, normed_in, qkv, down_shard, weights, tables):
    w_out, w_up, vectors, gains = weights
    staged = lax.axis_size("fsdp") == H
    attn_low, normed_one, scaled_one = normed_in
    width = features_in.shape[1]
    tokens = features_in.shape[0]
    starts, low, _ = tables
    halo = halo_count()
    if halo:
        qkv = jnp.concatenate([from_group(qkv, 1), qkv])
    if staged:
        pieces = gather_along_z(after(down_shard, qkv))
    mixed, mixed_f32, lse = attend(qkv, starts, low, halo)
    if staged:
        column, beside = gather_along_y([after(piece, lse) for piece in pieces])
    mixed = exchange(after(mixed, column) if staged else mixed)
    mixed = mixed.reshape(H * HD, tokens)
    if staged:
        plane, across = gather_across_cores(column, after(beside, mixed))
    else:
        w_down = lax.all_gather(down_shard, "fsdp", axis=0, tiled=True)
    residual = features_in + (contract(mixed, w_out, 0, 0) + vectors["out"])
    ffn_in, normed_two, scaled_two = layer_norm(residual, gains[width:], vectors["ln2"])
    ffn_low = ffn_in.astype(jnp.bfloat16)
    ffn_other = swap(ffn_low)
    up_own = contract(ffn_low, w_up, 1, 0) + vectors["up"]
    act_own = gelu_tanh(up_own).astype(jnp.bfloat16)
    if staged:
        ffn_other, act_own, across = lax.optimization_barrier((ffn_other, act_own, across))
        w_down = gathered_rows(plane, across)
    else:
        ffn_other, act_own = lax.optimization_barrier((ffn_other, act_own))
    up_other = contract(ffn_other, w_up, 1, 0) + vectors["up"]
    act_other = gelu_tanh(up_other).astype(jnp.bfloat16)
    arrived = swap(contract(act_other, w_down, 1, 0).astype(jnp.bfloat16))
    down_own = contract(act_own, w_down, 1, 0)
    unfinished = (residual + (down_own + vectors["down"]), arrived)
    kept = {
        "normed_one": normed_one,
        "scaled_one": scaled_one,
        "attn_low": attn_low,
        "qkv": qkv,
        "mixed": mixed,
        "mixed_f32": mixed_f32,
        "lse": lse,
        "normed_two": normed_two,
        "scaled_two": scaled_two,
        "ffn_both": jnp.concatenate([ffn_low, ffn_other]),
        "up_own": up_own,
        "up_other": up_other,
        "act_both": jnp.concatenate([act_own, act_other]),
        "w_down": w_down,
    }
    return unfinished, kept


def finish(unfinished, after):
    own, arrived = unfinished
    arrived, own, after = lax.optimization_barrier((arrived, own, after))
    return own + arrived.astype(jnp.float32), after


def scatter(grad):
    return lax.psum_scatter(grad.astype(jnp.bfloat16), "fsdp", scatter_dimension=0, tiled=True)


def shifted(value, axis_of, distance):
    count = lax.axis_size("fsdp")
    size, stride = {"z": (count // 4, 4), "y": (2, 2), "core": (2, 1)}[axis_of]

    def ahead(i):
        at = i // stride % size
        return i + ((at + distance) % size - at) * stride

    return lax.ppermute(value, "fsdp", [(i, ahead(i)) for i in range(count)])


def places():
    index = lax.axis_index("fsdp")
    return index // 4, index // 2 % 2, index % 2


def gather_along_z(shard):
    depth = lax.axis_size("fsdp") // 4
    return [shard] + [shifted(shard, "z", step) for step in range(1, depth)]


def gather_along_y(pieces):
    z, _, _ = places()
    depth = len(pieces)
    column = jnp.zeros((depth,) + pieces[0].shape, pieces[0].dtype)
    for step, piece in enumerate(pieces):
        column = lax.dynamic_update_index_in_dim(column, piece, (z - step) % depth, 0)
    return column, shifted(column, "y", 1)


def gather_across_cores(column, beside):
    _, y, _ = places()
    plane = jnp.stack(
        [jnp.where(y == 0, column, beside), jnp.where(y == 0, beside, column)], axis=1
    )
    return plane, shifted(plane, "core", 1)


def gathered_rows(plane, across):
    _, _, core = places()
    whole = jnp.stack(
        [jnp.where(core == 0, plane, across), jnp.where(core == 0, across, plane)], axis=2
    )
    return whole.reshape((-1, whole.shape[-1]))


def after(value, *deps):
    return lax.optimization_barrier((value,) + deps)[0]


def across_cores(full):
    _, _, core = places()
    depth = lax.axis_size("fsdp") // 4
    grid = full.reshape(depth, 2, 2, -1, full.shape[1])
    sent = jnp.where(core == 0, grid[:, :, 1], grid[:, :, 0])
    kept = jnp.where(core == 0, grid[:, :, 0], grid[:, :, 1])
    return kept, shifted(sent, "core", 1)


def across_y(kept, came):
    _, y, _ = places()

    def summed(side):
        part = jnp.where(side == 0, kept[:, 0], kept[:, 1]).astype(jnp.float32)
        return part + jnp.where(side == 0, came[:, 0], came[:, 1]).astype(jnp.float32)

    return summed(y), shifted(summed(1 - y).astype(jnp.bfloat16), "y", 1)


def across_z(kept, came):
    z, _, _ = places()
    depth = kept.shape[0]
    column = (kept + came.astype(jnp.float32)).astype(jnp.bfloat16)

    def at(step):
        return lax.dynamic_index_in_dim(column, (z + step) % depth, 0, keepdims=False)

    return [at(0)] + [shifted(at(step), "z", step) for step in range(1, depth)]


def summed_rows(pieces):
    total = pieces[0].astype(jnp.float32)
    for piece in pieces[1:]:
        total = total + piece.astype(jnp.float32)
    return total.astype(jnp.bfloat16)


def section_backward(incoming, incoming_other, kept, w_qkv, weights, tables, attn_all=None):
    w_out, w_up, _, gains = weights
    w_down = kept["w_down"]
    tokens, width = incoming.shape
    starts, low, high = tables
    halo = halo_count()

    def up_grad(rows, up_proj):
        act_grad = contract(rows, w_down, 1, 1)
        return jax.vjp(gelu_tanh, up_proj)[1](act_grad)[0].astype(jnp.bfloat16)

    up_own = up_grad(incoming, kept["up_own"])
    incoming_other, up_own = lax.optimization_barrier((incoming_other, up_own))
    up_other = up_grad(incoming_other, kept["up_other"])
    arrived = swap(contract(up_other, w_up, 1, 1).astype(jnp.bfloat16))
    partial = contract(up_own, w_up, 1, 1)
    up_low = jnp.concatenate([up_own, up_other])
    both = jnp.concatenate([incoming, incoming_other])
    grad_up = contract(kept["ffn_both"], up_low, 0, 0).astype(jnp.bfloat16)
    full_down = contract(kept["act_both"], both, 0, 0).astype(jnp.bfloat16)
    arrived, partial = lax.optimization_barrier((arrived, partial, grad_up, full_down))[:2]
    staged = lax.axis_size("fsdp") == H
    if staged:
        down_kept, down_came = across_cores(full_down)
    ffn_grad = partial + arrived.astype(jnp.float32)
    resid_norm, gain_two, shift_two = norm_back(
        ffn_grad, kept["normed_two"], kept["scaled_two"], gains[width:]
    )
    resid_grad = incoming.astype(jnp.float32) + resid_norm
    proj_low = resid_grad.astype(jnp.bfloat16)
    mixed_grad = contract(w_out, proj_low, 1, 1).astype(jnp.bfloat16)
    if staged:
        down_kept, down_came = across_y(down_kept, after(down_came, mixed_grad))
    mixed_grad = exchange(mixed_grad.reshape(H, HD, tokens))
    grad_out = contract(kept["mixed"], proj_low, 1, 0).astype(jnp.bfloat16)
    grad_mid = jnp.concatenate([grad_out, grad_up], axis=1)
    mixed_grad = after(mixed_grad, grad_mid)
    grad_mid = scatter(grad_mid)
    if staged:
        grad_down = across_z(down_kept, after(down_came, mixed_grad))
    else:
        grad_down = [scatter(full_down)]
    dqkv = attend_back(
        kept["qkv"], starts, low, high, mixed_grad, kept["mixed_f32"], kept["lse"], halo
    )
    if halo:
        behind = from_group(dqkv[:halo], -1).astype(jnp.float32)
        behind = behind.at[:, :HD].set(0.0)
        dqkv = (dqkv[halo:].astype(jnp.float32) + behind).astype(jnp.bfloat16)
    own_head = dqkv
    dqkv = from_heads(exchange(dqkv), tokens)
    if staged:
        dqkv = after(dqkv, *grad_down)
    attn_grad = contract(dqkv, w_qkv, 0, 1)
    if attn_all is None:
        grad_qkv = scatter(contract(kept["attn_low"], dqkv, 0, 1))
    else:
        dims = (((0, 2), (0, 1)), ((), ()))
        grad_head = lax.dot_general(own_head, attn_all, dims, preferred_element_type=jnp.float32)
        grad_qkv = grad_head
    qkv_bias = jnp.sum(dqkv, axis=1, dtype=jnp.float32)
    input_norm, gain_one, shift_one = norm_back(
        attn_grad, kept["normed_one"], kept["scaled_one"], gains[:width]
    )
    vector_grad = {
        "ln1": shift_one,
        "ln2": shift_two,
        "q": qkv_bias[:width],
        "v": qkv_bias[2 * width :],
        "out": jnp.sum(proj_low, axis=0, dtype=jnp.float32),
        "up": jnp.sum(up_low, axis=0, dtype=jnp.float32),
        "down": jnp.sum(incoming, axis=0, dtype=jnp.float32),
        "gains": jnp.concatenate([gain_one, gain_two]),
    }
    return resid_grad + input_norm, (grad_qkv, grad_mid, grad_down), vector_grad


def whole_step(x_in, cotangent, segment, w_qkv, w_out, w_up, w_down, vectors, gains):
    pipe_index = lax.axis_index("pipe")
    fsdp_index = lax.axis_index("fsdp")
    count = lax.axis_size("fsdp")
    first = pipe_index == 0
    _, _, width = x_in.shape
    hidden = w_up.shape[2]
    half = hidden // count // 2

    def mine(pair):
        return jnp.where(first, pair[0], pair[1])

    def other(pair):
        return jnp.where(first, pair[1], pair[0])

    def by_section(own, received):
        return jnp.where(first, own, received), jnp.where(first, received, own)

    up_halves = w_up[0].reshape(-1, count, 2, half)
    up_halves = [up_halves[:, :, side].reshape(-1, count * half) for side in range(2)]
    down_halves = [w_down[0, :half], w_down[0, half:]]
    small = jnp.concatenate([vectors[0], gains[0]])
    qkv_shards = by_section(w_qkv[0], swap(w_qkv[0]))
    mid_own = jnp.concatenate([w_out[0], mine(up_halves)], axis=1)
    mid_sent = jnp.concatenate([w_out[0], other(up_halves)], axis=1)
    mid_shards = by_section(mid_own, swap(mid_sent))
    down_shards = by_section(mine(down_halves), swap(other(down_halves)))
    small_shards = by_section(small, swap(small))

    seg_own = mine((segment[0], segment[1]))
    packed = jnp.concatenate([small_shards[0], small_shards[1], seg_own.astype(jnp.bfloat16)])
    packed = lax.all_gather(packed, "fsdp")
    lengths = small.shape[0]
    vec_rows = vectors.shape[1]
    segments = packed[:, 2 * lengths :].astype(jnp.int32)
    tables = doc_tables(segments, fsdp_index)

    def section_weights(section):
        piece = packed[:, section * lengths : (section + 1) * lengths].astype(jnp.float32)
        flat = piece[:, :vec_rows].reshape(-1)
        up_bias = flat[5 * width : 5 * width + hidden].reshape(count, 2, half)
        named = {
            "ln1": flat[:width],
            "ln2": flat[width : 2 * width],
            "q": flat[2 * width : 3 * width],
            "v": flat[3 * width : 4 * width],
            "out": flat[4 * width : 5 * width],
            "up": mine((up_bias[:, 0].reshape(-1), up_bias[:, 1].reshape(-1))),
            "down": flat[5 * width + hidden :],
        }
        gain_all = piece[:, vec_rows:].reshape(-1)
        full_mid = lax.all_gather(mid_shards[section], "fsdp", axis=0, tiled=True)
        return full_mid[:, :width], full_mid[:, width:], named, gain_all

    start_low = mine((x_in[0], x_in[1]))
    start_all = lax.all_gather(start_low, "fsdp", axis_index_groups=head_groups())
    w_head = spread_head_columns(qkv_shards[0])
    weights = [section_weights(0), section_weights(1)]
    w_qkv_one = lax.all_gather(qkv_shards[1], "fsdp", axis=0, tiled=True)
    w_qkv_zero = lax.all_gather(qkv_shards[0], "fsdp", axis=0, tiled=True)

    def normed(features, section):
        named, gain_all = weights[section][2:]
        attn_in, normed_one, scaled_one = layer_norm(features, gain_all[:width], named["ln1"])
        return attn_in.astype(jnp.bfloat16), normed_one, scaled_one

    attn_all = normed(start_all.astype(jnp.float32), 0)[0]
    qkv_zero = heads_of_group(attn_all, w_head, weights[0][2], fsdp_index % H)
    start = start_low.astype(jnp.float32)
    normed_start = normed(start, 0)
    unfinished_zero, kept_zero = section_forward(
        start, normed_start, qkv_zero, down_shards[0], weights[0], tables
    )
    result_zero = finish(unfinished_zero, ())[0]
    low_zero = result_zero.astype(jnp.bfloat16)
    middle = low_zero.astype(jnp.float32)
    normed_middle = normed(middle, 1)
    qkv_one = heads_from_tokens(normed_middle[0], w_qkv_one, weights[1][2])
    unfinished_one, kept_one = section_forward(
        middle, normed_middle, qkv_one, down_shards[1], weights[1], tables
    )

    pair = (cotangent[0], cotangent[1])
    grad_one, params_one, vecs_one = section_backward(
        mine(pair), other(pair), kept_one, w_qkv_one, weights[1], tables
    )
    grad_one = grad_one.astype(jnp.bfloat16)
    result_one, grad_one = finish(unfinished_one, grad_one)
    low_one = result_one.astype(jnp.bfloat16)
    grad_zero, params_zero, vecs_zero = section_backward(
        grad_one, swap(grad_one), kept_zero, w_qkv_zero, weights[0], tables, attn_all
    )
    grad_zero = grad_zero.astype(jnp.bfloat16)
    down_one = summed_rows(params_one[2])
    down_zero = summed_rows(params_zero[2])

    def both_batches(zero, one):
        kept_rows = mine((zero, one))
        came = swap(other((zero, one)))
        return jnp.stack([jnp.where(first, kept_rows, came), jnp.where(first, came, kept_rows)])[None]

    section_out = both_batches(low_zero, low_one)
    section_in_grad = both_batches(grad_zero, grad_one)

    def owned(zero, one):
        return mine((zero, one)), swap(other((zero, one)))

    def flat_vectors(named):
        up_half = named["up"].reshape(count, half)
        blank = jnp.zeros_like(up_half)
        up_all = jnp.stack([jnp.where(first, up_half, blank), jnp.where(first, blank, up_half)], axis=1)
        flat = jnp.concatenate(
            [named[key] for key in ("ln1", "ln2", "q", "v", "out")] + [up_all.reshape(-1), named["down"]]
        )
        return jnp.concatenate([flat.reshape(count, -1), named["gains"].reshape(count, -1)], axis=1)

    small_grads = jnp.concatenate([flat_vectors(vecs_zero), flat_vectors(vecs_one)], axis=1)
    qkv_zero_grad, small_grads = collect_head_columns(params_zero[0], small_grads)
    qkv_mine, qkv_came = owned(qkv_zero_grad, params_one[0])
    mid_mine, mid_came = owned(params_zero[1], params_one[1])
    down_mine, down_came = owned(down_zero, down_one)
    grad_qkv = qkv_mine.astype(jnp.float32) + qkv_came.astype(jnp.float32)
    grad_out = mid_mine[:, :width].astype(jnp.float32) + mid_came[:, :width].astype(jnp.float32)

    def woven(kept_half, came_half):
        return jnp.where(first, kept_half, came_half), jnp.where(first, came_half, kept_half)

    rows = w_up.shape[1]
    up_pair = woven(mid_mine[:, width:], mid_came[:, width:])
    grad_up = jnp.stack([part.reshape(rows, count, half) for part in up_pair], axis=2)
    grad_up = grad_up.reshape(rows, hidden).astype(jnp.float32)
    grad_down = jnp.concatenate(woven(down_mine, down_came)).astype(jnp.float32)

    small_mine, small_came = owned(small_grads[:lengths], small_grads[lengths:])
    small_total = small_mine + small_came
    return (
        section_out,
        section_in_grad,
        grad_qkv[None],
        grad_out[None],
        grad_up[None],
        grad_down[None],
        small_total[None, :vec_rows],
        small_total[None, vec_rows:],
    )


def solution(mesh):
    return jax.shard_map(
        whole_step,
        mesh=mesh,
        in_specs=(
            P(None, "fsdp", None),
            P(None, "fsdp", None),
            P(None, "fsdp"),
            P("pipe", "fsdp", None),
            P("pipe", "fsdp", None),
            P("pipe", "fsdp", None),
            P("pipe", "fsdp", None),
            P("pipe", "fsdp"),
            P("pipe", "fsdp"),
        ),
        out_specs=(
            P("pipe", None, "fsdp", None),
            P("pipe", None, "fsdp", None),
            P("pipe", "fsdp", None),
            P("pipe", "fsdp", None),
            P("pipe", "fsdp", None),
            P("pipe", "fsdp", None),
            P("pipe", "fsdp"),
            P("pipe", "fsdp"),
        ),
        check_vma=False,
    )
```
